32 devices in a mesh: pipe: 4 (over z), seq: 4 (over y, x), exp: 2 (over core).
Axes of the slice: x: 2, y: 2, z: 4, core: 2. Of those that a mesh axis runs over, the one named last changes fastest.
Arguments:
- queries: bfloat16 [4, 2, 512, 4096], P('pipe', 'exp', 'seq'), may hold values from -160 to 160
- key_rows: bfloat16 [4, 2, 512, 256], P('pipe', 'exp', 'seq'), may hold values from -160 to 160
- value_rows: bfloat16 [4, 2, 512, 256], P('pipe', 'exp', 'seq'), may hold values from -6 to 6
- residual: bfloat16 [4, 2, 512, 4096], P('pipe', 'exp', 'seq'), may hold values from -6 to 6
- doc_lengths: int32 [4, 2, 8], P('pipe', 'exp'), may hold values from 1 to 128, 512 in all within a row
- norm_gain: float32 [4, 4096], P('pipe'), may hold values from 0.1 to 1.9
- kv_weight: bfloat16 [4, 4096, 512], P('pipe', ('seq', 'exp')), may hold values from -0.09375 to 0.09375
Outputs:
- context: bfloat16 [4, 2, 512, 4096], P('pipe', 'exp', 'seq')
- kv_next: bfloat16 [4, 2, 512, 512], P('pipe', 'exp', 'seq')
The draws below stay inside these ranges and needn't reach their ends.
Inputs may be any that keep to these rules, and one draw needn't show every extreme that they name: `doc_lengths`: every pack has a document of exactly 128 tokens and none longer.
All inputs are finite; a program needn't handle non-finite values.
Results may differ from the reference program's by a relative error of at most 0.0058.
Values may be sent and summed in bfloat16 or wider, within the bound.
No kernel may reach another device: no remote copies, remote signals or barrier semaphores. Data moves between devices by JAX's collectives and lax.ppermute only.
A program may use at most 64 MiB of HBM per device.

```python
import math
import jax
import jax.numpy as jnp
import numpy as np
from jax import lax

HQ = 32
KVH = 2
DH = 128
NDOC = 8
TOK_DEV = 128
SEGMENTS = 4
PACKS = 2
SHARDS = 4
SEQ_TOK = 512
MOST = 128


def paired_heads(key):
    key_draw = jax.random.normal(jax.random.fold_in(key, 11), (SEGMENTS, PACKS, SEQ_TOK, KVH, DH), jnp.float32)
    query_draw = jax.random.normal(jax.random.fold_in(key, 12), (SEGMENTS, PACKS, SEQ_TOK, HQ, DH), jnp.float32)
    return (query_draw, key_draw)


def draw_queries(key, part):
    query_draw, key_draw = paired_heads(key)
    return query_draw.reshape(SEGMENTS, PACKS, SEQ_TOK, HQ * DH).astype(jnp.bfloat16)


def draw_key_rows(key, part):
    query_draw, key_draw = paired_heads(key)
    return key_draw.reshape(SEGMENTS, PACKS, SEQ_TOK, KVH * DH).astype(jnp.bfloat16)


def block_levels(stream_key, extent, cuts, low, largest):
    def one(axis_at, shards_of):
        heights = jax.random.uniform(jax.random.fold_in(jax.random.fold_in(stream_key, 6), axis_at), (shards_of,), jnp.float32, low / len(cuts), largest / len(cuts))
        return jnp.repeat(jnp.exp(heights), extent[axis_at] // shards_of).reshape((-1,) + (1,) * (len(extent) - axis_at - 1))

    loudness = one(*cuts[0])
    for cut in cuts[1:]:
        loudness = loudness * one(*cut)
    return loudness


def profile(count, total, most, lean):
    weights = [(1 << 20) // math.isqrt(grade ** lean) + 1 for grade in range(2, count + 1)]
    spare, counts = total - most - (count - 1), [1] * (count - 1)
    while spare > 0:
        movable = [i for i in range(count - 1) if counts[i] < most]
        pool, budget = sum([weights[i] for i in movable]), spare
        for i in movable:
            more = min(most - counts[i], max(1, budget * weights[i] // pool), spare)
            counts[i] = counts[i] + more
            spare = spare - more
    return np.array([most] + counts)


def uneven_parts(own_key, amount, total, bound, skew):
    if amount == 2:
        one = jax.random.randint(own_key, (), max(1, total - bound), min(bound, total - 1) + 1)
        return jnp.stack([one, total - one])
    sizes = jnp.asarray(profile(amount, total, bound, skew), jnp.int32)
    twos = (amount - 1) // 2
    giver, taker = sizes[1:1 + 2 * twos:2], sizes[2:2 + 2 * twos:2]
    room = jnp.minimum(giver - 1, bound - taker)
    passed = jax.random.randint(jax.random.fold_in(own_key, 1), (twos,), 0, 1 << 20) % (room + 1)
    sizes = sizes.at[1:1 + 2 * twos:2].set(giver - passed).at[2:2 + 2 * twos:2].set(taker + passed)
    return sizes[jax.random.permutation(jax.random.fold_in(own_key, 2), amount)]


def scatter_about(rng, extent, scale, bound, split=(), kind=jnp.bfloat16):
    array = scale * jax.random.normal(rng, extent, jnp.float32)
    if split:
        array = array * block_levels(rng, extent, split, -0.22, 0.18)
    return jnp.clip(array, -bound, bound).astype(kind)


def setup_inputs(seed: int = 0) -> dict:
    key_list = jax.random.split(jax.random.key(seed), 8)
    queries = draw_queries(jax.random.fold_in(key_list[7], 71), 0)
    key_rows = draw_key_rows(jax.random.fold_in(key_list[7], 71), 0)
    value_rows = scatter_about(key_list[2], (SEGMENTS, PACKS, SEQ_TOK, KVH * DH), 1.0, 6.0, ((0, 4), (1, 2), (2, 4)))
    residual = scatter_about(key_list[3], (SEGMENTS, PACKS, SEQ_TOK, HQ * DH), 1.0, 6.0, ((0, 4), (1, 2), (2, 4)))
    doc_lengths = jax.vmap(lambda own: uneven_parts(own, NDOC, SEQ_TOK, MOST, 2))(jax.random.split(key_list[4], SEGMENTS * PACKS)).reshape((SEGMENTS, PACKS, NDOC)).astype(jnp.int32)
    norm_gain = jnp.clip(1.0 + 0.18 * jax.random.normal(key_list[5], (SEGMENTS, HQ * DH), jnp.float32), 0.1, 1.9)
    kv_weight = scatter_about(key_list[6], (SEGMENTS, HQ * DH, 2 * KVH * DH), (HQ * DH) ** -0.5, 0.09375, ((0, 4), (1, 8)))
    return {"queries": queries, "key_rows": key_rows, "value_rows": value_rows, "residual": residual, "doc_lengths": doc_lengths, "norm_gain": norm_gain, "kv_weight": kv_weight}


epsilon = 1e-06

def storage_positions(seq_rows, tok_rows, groups):
    index = jnp.arange(seq_rows, dtype=jnp.int32)
    half_rows = tok_rows // 2
    owner_dev = index // tok_rows
    within = index % tok_rows
    return jnp.where(within < half_rows, owner_dev * half_rows + within, (2 * groups - 1 - owner_dev) * half_rows + within - half_rows).astype(jnp.int32)

def reference(queries, key_rows, value_rows, residual, doc_lengths, norm_gain, kv_weight):
    positions = storage_positions(SEQ_TOK, TOK_DEV, SHARDS)
    head_group = HQ // KVH
    score_scale = 1.0 / math.sqrt(DH)
    query_all = queries.reshape(SEGMENTS * PACKS, SEQ_TOK, HQ, DH)
    key_all = key_rows.reshape(SEGMENTS * PACKS, SEQ_TOK, KVH, DH)
    value_all = value_rows.reshape(SEGMENTS * PACKS, SEQ_TOK, KVH, DH)
    length_all = doc_lengths.reshape(SEGMENTS * PACKS, NDOC)

    def one_pack(packed):
        query_pack, key_pack, value_pack, lengths = packed
        bounds = jnp.cumsum(lengths)
        doc_ids = lax.optimization_barrier(jnp.sum((positions[:, None] >= bounds[None, :]).astype(jnp.int32), axis=1))
        visible = (doc_ids[:, None] == doc_ids[None, :]) & (positions[None, :] <= positions[:, None])

        def one_head(head):
            query_head = lax.dynamic_index_in_dim(query_pack, head, 1, keepdims=False)
            key_head = lax.dynamic_index_in_dim(key_pack, head // head_group, 1, keepdims=False)
            value_head = lax.dynamic_index_in_dim(value_pack, head // head_group, 1, keepdims=False)
            scores = jnp.dot(query_head, key_head.T, preferred_element_type=jnp.float32) * score_scale
            scores = jnp.where(visible, scores, -1e+30)
            row_max = lax.optimization_barrier(jnp.max(scores, axis=1, keepdims=True))
            weights = jnp.where(visible, jnp.exp(scores - row_max), 0.0)
            sums = lax.optimization_barrier(jnp.sum(weights, axis=1, keepdims=True))
            mixed_rows = jnp.dot(weights.astype(jnp.bfloat16), value_head, preferred_element_type=jnp.float32)
            return (mixed_rows / sums).astype(jnp.bfloat16)
        heads_out = lax.map(one_head, jnp.arange(HQ, dtype=jnp.int32))
        return jnp.transpose(heads_out, (1, 0, 2)).reshape(SEQ_TOK, HQ * DH)
    context = lax.map(one_pack, (query_all, key_all, value_all, length_all))
    context = context.reshape(SEGMENTS, PACKS, SEQ_TOK, HQ * DH)
    layer_out = (residual.astype(jnp.float32) + context.astype(jnp.float32)).astype(jnp.bfloat16)
    received = jnp.concatenate([jnp.zeros_like(layer_out[:1]), layer_out[:-1]], axis=0)
    as_float = received.astype(jnp.float32)
    mean_square = lax.optimization_barrier(jnp.mean(as_float * as_float, axis=3, keepdims=True))
    normed = (as_float * lax.rsqrt(mean_square + epsilon) * norm_gain[:, None, None, :]).astype(jnp.bfloat16)

    def project(packed):
        normed_segment, weight_segment = packed
        return jnp.dot(normed_segment, weight_segment, preferred_element_type=jnp.float32).astype(jnp.bfloat16)
    kv_next = lax.map(project, (normed.reshape(SEGMENTS, PACKS * SEQ_TOK, HQ * DH), kv_weight))
    return (context, kv_next.reshape(SEGMENTS, PACKS, SEQ_TOK, 2 * KVH * DH))
```

```python
import functools
import math

import jax
import jax.numpy as jnp
from jax import lax
from jax.experimental import pallas as pl
from jax.experimental.pallas import tpu as pltpu
from jax.sharding import PartitionSpec as P

DH = 128


epsilon = 1e-06
MASKED = -1e30


def shifted(block, distance):
    devices = range(lax.axis_size("pipe"))
    route = [(i - distance, i) for i in devices if i - distance in devices]
    return lax.ppermute(block, "pipe", route)


def shifted_across(block, distance):
    sections = range(lax.axis_size("pipe"))
    route = [
        ((i - distance) * 2 + c, i * 2 + 1 - c) for i in sections if i - distance in sections for c in range(2)
    ]
    return lax.ppermute(block, ("pipe", "exp"), route)


def exchanged(block, axis, bit):
    return lax.ppermute(block, axis, [(i, i ^ bit) for i in range(lax.axis_size(axis))])


def split_kernel(key_ref, value_ref, weight_ref, pair_ref, keep_ref, give_ref, sems):
    half = weight_ref.shape[1] // 2
    width = key_ref.shape[1]
    core = lax.axis_index("exp")
    mine = pl.ds(pl.multiple_of(core * half, half), half)
    other = pl.ds(pl.multiple_of((1 - core) * half, half), half)
    copies = [
        pltpu.make_async_copy(weight_ref.at[:, mine], keep_ref, sems.at[0]),
        pltpu.make_async_copy(weight_ref.at[:, other], give_ref, sems.at[1]),
        pltpu.make_async_copy(key_ref, pair_ref.at[:, :width], sems.at[2]),
        pltpu.make_async_copy(value_ref, pair_ref.at[:, width:], sems.at[3]),
    ]
    for copy in copies:
        copy.start()
    for copy in copies:
        copy.wait()


def split_local(key_rows, value_rows, weight):
    rows, width = key_rows.shape
    depth, cols = weight.shape
    piece = jax.ShapeDtypeStruct((depth, cols // 2), weight.dtype)
    return pl.pallas_call(
        split_kernel,
        out_shape=(jax.ShapeDtypeStruct((rows, 2 * width), key_rows.dtype), piece, piece),
        in_specs=[pl.BlockSpec(memory_space=pl.ANY)] * 3,
        out_specs=(pl.BlockSpec(memory_space=pltpu.VMEM),) * 3,
        scratch_shapes=[pltpu.SemaphoreType.DMA((4,))],
        name="split_local",
    )(key_rows, value_rows, weight)


def attend_kernel(
    groups, longest, score_scale, lengths_ref, query_ref, residual_ref, gain_ref, *refs
):
    pair_refs, (context_ref, normed_ref, every, layer) = refs[:-4], refs[-4:]
    tok_rows, row_width = query_ref.shape
    half_rows = tok_rows // 2
    kv_width = every.shape[2] // 2
    kv_heads = kv_width // DH
    heads = row_width // DH
    per_kv = heads // kv_heads
    window = longest + half_rows
    blocks = window // half_rows
    own = lax.axis_index("seq")
    if len(pair_refs) == 1:
        every[...] = pair_refs[0][...].reshape(every.shape)
    else:
        for bit, pair_ref in enumerate(pair_refs):
            every[own ^ bit] = pair_ref[...]
    bounds = []
    total = jnp.int32(0)
    for doc in range(lengths_ref.shape[1]):
        total = total + lengths_ref[0, doc]
        bounds.append(total)
    exponent = score_scale * math.log2(math.e)
    for run in range(2):
        block = own if run == 0 else 2 * groups - 1 - own
        first_pos = block * half_rows
        rows = slice(run * half_rows, (run + 1) * half_rows)
        query_pos = first_pos + lax.broadcasted_iota(jnp.int32, (half_rows, window), 0)
        key_pos = first_pos + half_rows - window + lax.broadcasted_iota(jnp.int32, (half_rows, window), 1)
        doc_start = jnp.zeros((half_rows, window), jnp.int32)
        for bound in bounds:
            doc_start = jnp.where(bound <= query_pos, bound, doc_start)
        visible = (doc_start <= key_pos) & (key_pos <= query_pos)
        key_parts, value_parts = [], []
        for back in range(blocks - 1, -1, -1):
            natural = jnp.maximum(block - back, 0)
            second = natural >= groups
            owner = jnp.where(second, 2 * groups - 1 - natural, natural)
            offset = jnp.where(second, half_rows, 0)
            part = every[owner, pl.ds(pl.multiple_of(offset, half_rows), half_rows), :]
            key_parts.append(part[:, :kv_width])
            value_parts.append(part[:, kv_width:])
        key_win = jnp.concatenate(key_parts, axis=0)
        value_win = jnp.concatenate(value_parts, axis=0)
        squares = jnp.zeros((half_rows, DH), jnp.float32)
        for group in range(kv_heads):
            lanes = slice(group * DH, (group + 1) * DH)
            query_stack = jnp.concatenate(
                [
                    query_ref[rows, (group * per_kv + h) * DH : (group * per_kv + h + 1) * DH]
                    for h in range(per_kv)
                ],
                axis=0,
            )
            scores = lax.dot_general(
                query_stack, key_win[:, lanes], (((1,), (1,)), ((), ())), preferred_element_type=jnp.float32
            )
            masked = jnp.where(visible[None], scores.reshape(per_kv, half_rows, window), MASKED)
            row_max = jnp.max(masked, axis=2, keepdims=True)
            weights = jnp.exp2((masked - row_max) * exponent)
            sums = jnp.sum(weights, axis=2, keepdims=True)
            rounded = weights.astype(jnp.bfloat16).reshape(per_kv * half_rows, window)
            mixed = jnp.dot(rounded, value_win[:, lanes], preferred_element_type=jnp.float32)
            context = (mixed.reshape(per_kv, half_rows, DH) / sums).astype(jnp.bfloat16)
            for h in range(per_kv):
                cols = slice((group * per_kv + h) * DH, (group * per_kv + h + 1) * DH)
                context_ref[rows, cols] = context[h]
                added = (
                    residual_ref[rows, cols].astype(jnp.float32) + context[h].astype(jnp.float32)
                ).astype(jnp.bfloat16)
                layer[rows, cols] = added
                wide = added.astype(jnp.float32)
                squares = squares + wide * wide
        mean_square = jnp.sum(squares, axis=1, keepdims=True) * (1.0 / row_width)
        inverse = lax.rsqrt(mean_square + epsilon)
        for head in range(heads):
            cols = slice(head * DH, (head + 1) * DH)
            normed_ref[rows, cols] = (
                layer[rows, cols].astype(jnp.float32) * inverse * gain_ref[:, cols]
            ).astype(jnp.bfloat16)


def attend(lengths, queries, residual, gain, pairs, groups):
    tok_rows, row_width = queries.shape
    longest = tok_rows * groups // 4
    pair_width = pairs[0].shape[1]
    whole = pl.BlockSpec(memory_space=pltpu.VMEM)
    shape = jax.ShapeDtypeStruct(queries.shape, jnp.bfloat16)
    return pl.pallas_call(
        functools.partial(attend_kernel, groups, longest, 1.0 / math.sqrt(DH)),
        out_shape=(shape, shape),
        in_specs=[pl.BlockSpec(memory_space=pltpu.SMEM)] + [whole] * (3 + len(pairs)),
        out_specs=(whole, whole),
        scratch_shapes=[
            pltpu.VMEM((groups, tok_rows, pair_width), jnp.bfloat16),
            pltpu.VMEM((tok_rows, row_width), jnp.bfloat16),
        ],
        name="attend",
    )(lengths, queries, residual, gain, *pairs)


def project_kernel(own_ref, other_ref, *refs):
    piece_refs, (same_ref, cross_ref) = refs[:-2], refs[-2:]
    depth = piece_refs[0].shape[0]
    seq, core = lax.axis_index("seq"), lax.axis_index("exp")
    totals = [None, None]
    for at, piece_ref in enumerate(piece_refs):
        bit, kind = at // 2, at % 2
        column = ((seq ^ bit) * 2 + (core ^ kind)) * depth
        cols = pl.ds(pl.multiple_of(column, depth), depth)
        piece = piece_ref[...]
        for token, ref in enumerate((own_ref, other_ref)):
            part = jnp.dot(ref[:, cols], piece, preferred_element_type=jnp.float32)
            totals[token] = part if totals[token] is None else totals[token] + part
    same_ref[...] = totals[0].astype(jnp.bfloat16)
    cross_ref[...] = totals[1].astype(jnp.bfloat16)


def project(normed, normed_other, pieces):
    whole = pl.BlockSpec(memory_space=pltpu.VMEM)
    shape = jax.ShapeDtypeStruct((normed.shape[0], pieces[0].shape[1]), jnp.bfloat16)
    return pl.pallas_call(
        project_kernel,
        out_shape=(shape, shape),
        in_specs=[whole] * (2 + len(pieces)),
        out_specs=(whole, whole),
        name="project",
    )(normed, normed_other, *pieces)


def square_of_chips(queries, key_rows, value_rows, residual, lengths, norm_gain, weight):
    groups = lax.axis_size("seq")
    gain = shifted(norm_gain, -1)
    pair, keep, give = split_local(key_rows, value_rows, weight)
    pairs = [pair] + [exchanged(pair, "seq", bit) for bit in (1, 2, 3)]
    kept = shifted(keep, -1)
    given = shifted(exchanged(give, "exp", 1), -1)
    kept_x, kept_y = exchanged(kept, "seq", 1), exchanged(kept, "seq", 2)
    given_x, given_y = exchanged(given, "seq", 1), exchanged(given, "seq", 2)
    kept_d = exchanged(kept_x, "seq", 2)
    given_d = exchanged(given_y, "seq", 1)
    context, normed = attend(lengths, queries, residual, gain, pairs, groups)
    normed_other = exchanged(normed, "exp", 1)
    same, cross = project(
        normed, normed_other, (kept, given, kept_x, given_x, kept_y, given_y, kept_d, given_d)
    )
    same_in, cross_in = shifted(same, 1), shifted_across(cross, 1)
    first = lax.axis_index("exp") == 0
    kv_next = jnp.concatenate(
        [jnp.where(first, same_in, cross_in), jnp.where(first, cross_in, same_in)], axis=1
    )
    return context, kv_next


def any_mesh(queries, key_rows, value_rows, residual, lengths, norm_gain, weight):
    groups = lax.axis_size("seq")
    gain = shifted(norm_gain, -1)
    weight_next = shifted(weight, -1)
    pair = jnp.concatenate([key_rows, value_rows], axis=1)
    pairs = [lax.all_gather(pair, "seq", axis=0, tiled=True)]
    context, normed = attend(lengths, queries, residual, gain, pairs, groups)
    every = lax.all_gather(weight_next, ("seq", "exp"), axis=0, tiled=True)
    projected = jnp.dot(normed, every, preferred_element_type=jnp.float32).astype(jnp.bfloat16)
    return context, shifted(projected, 1)


def on_device(queries, key_rows, value_rows, residual, doc_lengths, norm_gain, kv_weight):
    square = lax.axis_size("seq") == 4 and lax.axis_size("exp") == 2
    context, kv_next = (square_of_chips if square else any_mesh)(
        queries[0, 0], key_rows[0, 0], value_rows[0, 0], residual[0, 0], doc_lengths[0], norm_gain, kv_weight[0]
    )
    return context[None, None], kv_next[None, None]


def solution(mesh):
    rows = P("pipe", "exp", "seq", None)
    return jax.shard_map(
        on_device,
        mesh=mesh,
        in_specs=(rows, rows, rows, rows, P("pipe", "exp", None), P("pipe", None), P("pipe", ("seq", "exp"), None)),
        out_specs=(rows, rows),
        check_vma=False,
    )
```

```python
import functools
import math

import jax
import jax.numpy as jnp
from jax import lax
from jax.experimental import pallas as pl
from jax.experimental.pallas import tpu as pltpu
from jax.sharding import PartitionSpec as P


DH = 128


epsilon = 1e-06
MASKED = -1e30

WHOLE = pl.BlockSpec(memory_space=pltpu.VMEM)
FAR = pl.BlockSpec(memory_space=pltpu.HBM)


def near(array):
    return pltpu.with_memory_space_constraint(array, pltpu.VMEM)


def far(array):
    return pltpu.with_memory_space_constraint(array, pltpu.HBM)


def budget(mebibytes):
    return pltpu.CompilerParams(vmem_limit_bytes=mebibytes << 20)


def shifted(block, distance):
    devices = range(lax.axis_size("pipe"))
    route = [(i - distance, i) for i in devices if i - distance in devices]
    return lax.ppermute(block, "pipe", route)


def exchanged(block, axis, bit):
    return lax.ppermute(block, axis, [(i, i ^ bit) for i in range(lax.axis_size(axis))])


def run_copies(copies):
    for copy in copies:
        copy.start()
    for copy in copies:
        copy.wait()


def prepare_kernel(key_ref, value_ref, gain_ref, weight_ref, pair_ref, *refs):
    piece_refs, (weight, gain, sems) = refs[:-3], refs[-3:]
    width = key_ref.shape[1]
    depth = weight_ref.shape[0]
    at = (lax.axis_index("seq") * lax.axis_size("exp") + lax.axis_index("exp")) * depth
    run_copies(
        [
            pltpu.make_async_copy(weight_ref, weight, sems.at[0]),
            pltpu.make_async_copy(gain_ref, gain, sems.at[1]),
            pltpu.make_async_copy(key_ref, pair_ref.at[:, :width], sems.at[2]),
            pltpu.make_async_copy(value_ref, pair_ref.at[:, width:], sems.at[3]),
        ]
    )
    if depth % DH:
        wide = gain[...]
        place = lax.broadcasted_iota(jnp.int32, (depth, wide.shape[1]), 0) + at
        here = place == lax.broadcasted_iota(jnp.int32, place.shape, 1)
        column = jnp.sum(jnp.where(here, wide, 0.0), axis=1, keepdims=True)
    else:
        wide = gain[:, pl.ds(pl.multiple_of(at, depth), depth)]
        column = jnp.transpose(jnp.broadcast_to(wide, (DH, depth)))
    rows = depth // len(piece_refs)
    for index, piece_ref in enumerate(piece_refs):
        part = slice(index * rows, (index + 1) * rows)
        for left in range(0, weight.shape[1], DH):
            cols = slice(left, left + DH)
            piece_ref[:, cols] = (weight[part, cols].astype(jnp.float32) * column[part]).astype(jnp.bfloat16)


def prepare(key_rows, value_rows, norm_gain, weight, pieces):
    rows, width = key_rows.shape
    depth, cols = weight.shape
    piece = pltpu.VMEM((depth // pieces, cols), weight.dtype)
    return pl.pallas_call(
        prepare_kernel,
        out_shape=(pltpu.VMEM((rows, 2 * width), key_rows.dtype), *[piece] * pieces),
        in_specs=[FAR] * 4,
        out_specs=(WHOLE,) * (1 + pieces),
        scratch_shapes=[
            pltpu.VMEM((depth, cols), weight.dtype),
            pltpu.VMEM(norm_gain.shape, jnp.float32),
            pltpu.SemaphoreType.DMA((4,)),
        ],
        compiler_params=budget(6),
        name="prepare",
    )(*[far(array) for array in (key_rows, value_rows, norm_gain, weight)])


def fetch_kernel(*refs):
    count = (len(refs) - 1) // 2
    sems = refs[-1]
    run_copies(
        [pltpu.make_async_copy(refs[i], refs[count + i], sems.at[i]) for i in range(count)]
    )


def fetch(*arrays):
    return pl.pallas_call(
        fetch_kernel,
        out_shape=tuple(pltpu.VMEM(array.shape, array.dtype) for array in arrays),
        in_specs=[FAR] * len(arrays),
        out_specs=(WHOLE,) * len(arrays),
        scratch_shapes=[pltpu.SemaphoreType.DMA((len(arrays),))],
        compiler_params=budget(4),
        name="fetch",
    )(*[far(array) for array in arrays])


def attend_kernel(groups, longest, score_scale, far_lengths_ref, query_ref, residual_ref, *refs):
    pair_refs, (context_ref, layer_ref, inverse_ref, every, lengths_ref, sem) = refs[:-6], refs[-6:]
    lengths_copy = pltpu.make_async_copy(far_lengths_ref, lengths_ref, sem)
    lengths_copy.start()
    tok_rows, row_width = query_ref.shape
    half_rows = tok_rows // 2
    kv_width = every.shape[2] // 2
    kv_heads = kv_width // DH
    per_kv = row_width // DH // kv_heads
    window = longest + half_rows
    blocks = window // half_rows
    own = lax.axis_index("seq")
    if len(pair_refs) == 1:
        every[...] = pair_refs[0][...].reshape(every.shape)
    else:
        for bit, pair_ref in enumerate(pair_refs):
            every[own ^ bit] = pair_ref[...]
    lengths_copy.wait()
    bounds = []
    total = jnp.int32(0)
    for doc in range(lengths_ref.shape[1]):
        total = total + lengths_ref[0, doc]
        bounds.append(total)
    exponent = score_scale * math.log2(math.e)
    for run in range(2):
        block = own if run == 0 else 2 * groups - 1 - own
        first_pos = block * half_rows
        rows = slice(run * half_rows, (run + 1) * half_rows)
        query_pos = first_pos + lax.broadcasted_iota(jnp.int32, (half_rows, window), 0)
        key_pos = first_pos + half_rows - window + lax.broadcasted_iota(jnp.int32, (half_rows, window), 1)
        doc_start = jnp.zeros((half_rows, window), jnp.int32)
        for bound in bounds:
            doc_start = jnp.where(bound <= query_pos, bound, doc_start)
        visible = (doc_start <= key_pos) & (key_pos <= query_pos)
        key_parts, value_parts = [], []
        for back in range(blocks - 1, -1, -1):
            natural = jnp.maximum(block - back, 0)
            second = natural >= groups
            owner = jnp.where(second, 2 * groups - 1 - natural, natural)
            offset = jnp.where(second, half_rows, 0)
            part = every[owner, pl.ds(pl.multiple_of(offset, half_rows), half_rows), :]
            key_parts.append(part[:, :kv_width])
            value_parts.append(part[:, kv_width:])
        key_win = jnp.concatenate(key_parts, axis=0)
        value_win = jnp.concatenate(value_parts, axis=0)
        squares = jnp.zeros((half_rows, DH), jnp.float32)
        for group in range(kv_heads):
            lanes = slice(group * DH, (group + 1) * DH)
            query_stack = jnp.concatenate(
                [
                    query_ref[rows, (group * per_kv + h) * DH : (group * per_kv + h + 1) * DH]
                    for h in range(per_kv)
                ],
                axis=0,
            )
            scores = lax.dot_general(
                query_stack, key_win[:, lanes], (((1,), (1,)), ((), ())), preferred_element_type=jnp.float32
            )
            masked = jnp.where(visible[None], scores.reshape(per_kv, half_rows, window), MASKED)
            row_max = jnp.max(masked, axis=2, keepdims=True)
            weights = jnp.exp2((masked - row_max) * exponent)
            sums = jnp.sum(weights, axis=2, keepdims=True)
            rounded = weights.astype(jnp.bfloat16).reshape(per_kv * half_rows, window)
            mixed = jnp.dot(rounded, value_win[:, lanes], preferred_element_type=jnp.float32)
            context = (mixed.reshape(per_kv, half_rows, DH) / sums).astype(jnp.bfloat16)
            for h in range(per_kv):
                cols = slice((group * per_kv + h) * DH, (group * per_kv + h + 1) * DH)
                context_ref[rows, cols] = context[h]
                added = (
                    residual_ref[rows, cols].astype(jnp.float32) + context[h].astype(jnp.float32)
                ).astype(jnp.bfloat16)
                layer_ref[rows, cols] = added
                wide = added.astype(jnp.float32)
                squares = squares + wide * wide
        mean_square = jnp.sum(squares, axis=1, keepdims=True) * (1.0 / row_width)
        inverse_ref[rows, :] = jnp.broadcast_to(lax.rsqrt(mean_square + epsilon), (half_rows, DH))


def attend(lengths, queries, residual, pairs, groups):
    tok_rows, _ = queries.shape
    longest = tok_rows * groups // 4
    pair_width = pairs[0].shape[1]
    shape = pltpu.VMEM(queries.shape, jnp.bfloat16)
    return pl.pallas_call(
        functools.partial(attend_kernel, groups, longest, 1.0 / math.sqrt(DH)),
        out_shape=(shape, shape, pltpu.VMEM((tok_rows, DH), jnp.float32)),
        in_specs=[FAR] + [WHOLE] * (2 + len(pairs)),
        out_specs=(WHOLE,) * 3,
        scratch_shapes=[
            pltpu.VMEM((groups, tok_rows, pair_width), jnp.bfloat16),
            pltpu.SMEM(lengths.shape, jnp.int32),
            pltpu.SemaphoreType.DMA,
        ],
        compiler_params=budget(16),
        name="attend",
    )(far(lengths), *[near(array) for array in (queries, residual, *pairs)])


def project_kernel(places, last, layer_ref, *refs):
    piece_refs = refs[: len(places)]
    rest = refs[len(places) :]
    out_ref = rest[-1]
    depth = layer_ref.shape[1] // (lax.axis_size("seq") * lax.axis_size("exp"))
    seq, core = lax.axis_index("seq"), lax.axis_index("exp")
    total = None if len(rest) == 1 else rest[0][...]
    for (bit, kind, first), piece_ref in zip(places, piece_refs):
        rows = piece_ref.shape[0]
        column = ((seq ^ bit) * 2 + (core ^ kind)) * depth + first
        part = jnp.dot(
            layer_ref[:, pl.ds(pl.multiple_of(column, DH), rows)], piece_ref[...], preferred_element_type=jnp.float32
        )
        total = part if total is None else total + part
    if last:
        inverse_ref = rest[1]
        for left in range(0, total.shape[1], DH):
            cols = slice(left, left + DH)
            out_ref[:, cols] = (total[:, cols] * inverse_ref[...]).astype(jnp.bfloat16)
    else:
        out_ref[...] = total


def project(layer, held, so_far=None, inverse=None):
    places = tuple(held)
    last = inverse is not None
    blocks = [held[place] for place in places]
    extra = [array for array in (so_far, inverse) if array is not None]
    shape = (layer.shape[0], blocks[0].shape[1])
    return pl.pallas_call(
        functools.partial(project_kernel, places, last),
        out_shape=pltpu.VMEM(shape, jnp.bfloat16 if last else jnp.float32),
        in_specs=[WHOLE] * (1 + len(blocks) + len(extra)),
        out_specs=WHOLE,
        compiler_params=budget(8),
        name="project",
    )(*[near(array) for array in (layer, *blocks, *extra)])


def square_of_chips(queries, key_rows, value_rows, residual, lengths, norm_gain, weight):
    pair, *parts = prepare(key_rows, value_rows, norm_gain, weight, 2)
    early, late = {}, {}

    def hold(held, bit, first, block):
        held[bit, 0, first] = block
        held[bit, 1, first] = exchanged(block, "exp", 1)

    first = 0
    for index, part in enumerate(parts):
        block = shifted(part, -1)
        hold(early, 0, first, block)
        sides = {}
        for bit in (1, 2):
            sides[bit] = exchanged(block, "seq", bit)
            hold(early, bit, first, sides[bit])
        half = block.shape[0] // 2
        for bit in (1, 2):
            start = (bit - 1) * half
            corner = exchanged(sides[bit][start : start + half], "seq", 3 - bit)
            hold(early if index == 0 else late, 3, first + start, corner)
        first += block.shape[0]
    pairs = [pair]
    for bit in (1, 2, 3):
        pairs.append(exchanged(pair, "seq", bit))
    queries, residual = fetch(queries, residual)
    context, layer, inverse = attend(lengths, queries, residual, pairs, lax.axis_size("seq"))
    so_far = project(layer, early)
    projected = project(layer, late, so_far, inverse)
    return context, shifted(projected, 1)


def any_mesh(queries, key_rows, value_rows, residual, lengths, norm_gain, weight):
    pair, part = prepare(key_rows, value_rows, norm_gain, weight, 1)
    pairs = [lax.all_gather(pair, "seq", axis=0, tiled=True)]
    context, layer, inverse = attend(lengths, queries, residual, pairs, lax.axis_size("seq"))
    every = lax.all_gather(shifted(part, -1), ("seq", "exp"), axis=0, tiled=True)
    total = jnp.dot(layer, every, preferred_element_type=jnp.float32)
    return context, shifted((total * inverse[:, :1]).astype(jnp.bfloat16), 1)


def is_square(sizes):
    return sizes["seq"] == 4 and sizes["exp"] == 2


def on_device(queries, key_rows, value_rows, residual, doc_lengths, norm_gain, kv_weight):
    square = is_square({axis: lax.axis_size(axis) for axis in ("seq", "exp")})
    context, kv_next = (square_of_chips if square else any_mesh)(
        queries[0, 0], key_rows[0, 0], value_rows[0, 0], residual[0, 0], doc_lengths[0], norm_gain, kv_weight[0]
    )
    return context[None, None], kv_next[None, None]


def solution(mesh):
    rows = P("pipe", "exp", "seq", None)
    return jax.shard_map(
        on_device,
        mesh=mesh,
        in_specs=(rows, rows, rows, rows, P("pipe", "exp", None), P("pipe", None), P("pipe", ("seq", "exp"), None)),
        out_specs=(rows, rows),
        check_vma=False,
    )
```

```python
import functools
import math

import jax
import jax.numpy as jnp
from jax import lax
from jax.experimental import pallas as pl
from jax.experimental.pallas import tpu as pltpu
from jax.sharding import PartitionSpec as P


DH = 128


epsilon = 1e-06
MASKED = -1e30

WHOLE = pl.BlockSpec(memory_space=pltpu.VMEM)
FAR = pl.BlockSpec(memory_space=pltpu.HBM)


def near(array):
    return pltpu.with_memory_space_constraint(array, pltpu.VMEM)


def far(array):
    return pltpu.with_memory_space_constraint(array, pltpu.HBM)


def budget(mebibytes):
    return pltpu.CompilerParams(vmem_limit_bytes=mebibytes << 20)


def shifted(block, distance):
    devices = range(lax.axis_size("pipe"))
    route = [(i - distance, i) for i in devices if i - distance in devices]
    return lax.ppermute(block, "pipe", route)


def exchanged(block, axis, bit):
    return lax.ppermute(block, axis, [(i, i ^ bit) for i in range(lax.axis_size(axis))])


def run_copies(copies):
    for copy in copies:
        copy.start()
    for copy in copies:
        copy.wait()


def sent_half(device, groups):
    return (device >= groups // 2).astype(jnp.int32)


def prepare_kernel(key_ref, value_ref, gain_ref, weight_ref, pair_ref, half_ref, *refs):
    piece_refs, (weight, gain, sems) = refs[:-3], refs[-3:]
    half = half_ref.shape[0]
    sent = pl.ds(pl.multiple_of(sent_half(lax.axis_index("seq"), lax.axis_size("seq")) * half, half), half)
    width = key_ref.shape[1]
    depth = weight_ref.shape[0]
    at = (lax.axis_index("seq") * lax.axis_size("exp") + lax.axis_index("exp")) * depth
    run_copies(
        [
            pltpu.make_async_copy(weight_ref, weight, sems.at[0]),
            pltpu.make_async_copy(gain_ref, gain, sems.at[1]),
            pltpu.make_async_copy(key_ref, pair_ref.at[:, :width], sems.at[2]),
            pltpu.make_async_copy(value_ref, pair_ref.at[:, width:], sems.at[3]),
            pltpu.make_async_copy(key_ref.at[sent], half_ref.at[:, :width], sems.at[4]),
            pltpu.make_async_copy(value_ref.at[sent], half_ref.at[:, width:], sems.at[5]),
        ]
    )
    if depth % DH:
        wide = gain[...]
        place = lax.broadcasted_iota(jnp.int32, (depth, wide.shape[1]), 0) + at
        here = place == lax.broadcasted_iota(jnp.int32, place.shape, 1)
        column = jnp.sum(jnp.where(here, wide, 0.0), axis=1, keepdims=True)
    else:
        wide = gain[:, pl.ds(pl.multiple_of(at, depth), depth)]
        column = jnp.transpose(jnp.broadcast_to(wide, (DH, depth)))
    rows = depth // len(piece_refs)
    for index, piece_ref in enumerate(piece_refs):
        part = slice(index * rows, (index + 1) * rows)
        for left in range(0, weight.shape[1], DH):
            cols = slice(left, left + DH)
            piece_ref[:, cols] = (weight[part, cols].astype(jnp.float32) * column[part]).astype(jnp.bfloat16)


def prepare(key_rows, value_rows, norm_gain, weight, pieces):
    rows, width = key_rows.shape
    depth, cols = weight.shape
    piece = pltpu.VMEM((depth // pieces, cols), weight.dtype)
    return pl.pallas_call(
        prepare_kernel,
        out_shape=(
            pltpu.VMEM((rows, 2 * width), key_rows.dtype),
            pltpu.VMEM((rows // 2, 2 * width), key_rows.dtype),
            *[piece] * pieces,
        ),
        in_specs=[FAR] * 4,
        out_specs=(WHOLE,) * (2 + pieces),
        scratch_shapes=[
            pltpu.VMEM((depth, cols), weight.dtype),
            pltpu.VMEM(norm_gain.shape, jnp.float32),
            pltpu.SemaphoreType.DMA((6,)),
        ],
        compiler_params=budget(6),
        name="prepare",
    )(*[far(array) for array in (key_rows, value_rows, norm_gain, weight)])


def fetch_kernel(*refs):
    count = (len(refs) - 1) // 2
    sems = refs[-1]
    run_copies(
        [pltpu.make_async_copy(refs[i], refs[count + i], sems.at[i]) for i in range(count)]
    )


def fetch(*arrays):
    return pl.pallas_call(
        fetch_kernel,
        out_shape=tuple(pltpu.VMEM(array.shape, array.dtype) for array in arrays),
        in_specs=[FAR] * len(arrays),
        out_specs=(WHOLE,) * len(arrays),
        scratch_shapes=[pltpu.SemaphoreType.DMA((len(arrays),))],
        compiler_params=budget(4),
        name="fetch",
    )(*[far(array) for array in arrays])


def store_kernel(near_ref, far_ref, sem):
    run_copies([pltpu.make_async_copy(near_ref, far_ref, sem)])


def store(array):
    return pl.pallas_call(
        store_kernel,
        out_shape=jax.ShapeDtypeStruct(array.shape, array.dtype),
        in_specs=[WHOLE],
        out_specs=FAR,
        scratch_shapes=[pltpu.SemaphoreType.DMA],
        compiler_params=budget(2),
        name="store",
    )(near(array))


def attend_kernel(groups, longest, score_scale, stays, far_lengths_ref, query_ref, residual_ref, *refs):
    pair_refs, outs = refs[: -len(stays) - 5], refs[-len(stays) - 5 :]
    context_ref, inverse_ref, *layer_refs, every, lengths_ref, sem = outs
    lengths_copy = pltpu.make_async_copy(far_lengths_ref, lengths_ref, sem)
    lengths_copy.start()
    tok_rows, row_width = query_ref.shape
    half_rows = tok_rows // 2
    kv_width = every.shape[2] // 2
    kv_heads = kv_width // DH
    per_kv = row_width // DH // kv_heads
    window = longest + half_rows
    blocks = window // half_rows
    own = lax.axis_index("seq")
    if len(pair_refs) == 1:
        every[...] = pair_refs[0][...].reshape(every.shape)
    else:
        for bit, pair_ref in enumerate(pair_refs):
            sender, rows = own ^ bit, pair_ref.shape[0]
            if rows == tok_rows:
                every[sender] = pair_ref[...]
            else:
                at = pl.multiple_of(sent_half(sender, groups) * rows, rows)
                every[sender, pl.ds(at, rows), :] = pair_ref[...]
    lengths_copy.wait()
    bounds = []
    total = jnp.int32(0)
    for doc in range(lengths_ref.shape[1]):
        total = total + lengths_ref[0, doc]
        bounds.append(total)
    exponent = score_scale * math.log2(math.e)
    places = {head: (ref, at) for ref, heads in zip(layer_refs, stays) for at, head in enumerate(heads)}

    def put(rows, head, block):
        ref, at = places[head]
        ref[rows, at * DH : (at + 1) * DH] = block

    for run in range(2):
        block = own if run == 0 else 2 * groups - 1 - own
        first_pos = block * half_rows
        rows = slice(run * half_rows, (run + 1) * half_rows)
        query_pos = first_pos + lax.broadcasted_iota(jnp.int32, (half_rows, window), 0)
        key_pos = first_pos + half_rows - window + lax.broadcasted_iota(jnp.int32, (half_rows, window), 1)
        doc_start = jnp.zeros((half_rows, window), jnp.int32)
        for bound in bounds:
            doc_start = jnp.where(bound <= query_pos, bound, doc_start)
        visible = (doc_start <= key_pos) & (key_pos <= query_pos)
        key_parts, value_parts = [], []
        for back in range(blocks - 1, -1, -1):
            natural = jnp.maximum(block - back, 0)
            second = natural >= groups
            owner = jnp.where(second, 2 * groups - 1 - natural, natural)
            offset = jnp.where(second, half_rows, 0)
            part = every[owner, pl.ds(pl.multiple_of(offset, half_rows), half_rows), :]
            key_parts.append(part[:, :kv_width])
            value_parts.append(part[:, kv_width:])
        key_win = jnp.concatenate(key_parts, axis=0)
        value_win = jnp.concatenate(value_parts, axis=0)
        squares = jnp.zeros((half_rows, DH), jnp.float32)
        for group in range(kv_heads):
            lanes = slice(group * DH, (group + 1) * DH)
            query_stack = jnp.concatenate(
                [
                    query_ref[rows, (group * per_kv + h) * DH : (group * per_kv + h + 1) * DH]
                    for h in range(per_kv)
                ],
                axis=0,
            )
            scores = lax.dot_general(
                query_stack, key_win[:, lanes], (((1,), (1,)), ((), ())), preferred_element_type=jnp.float32
            )
            masked = jnp.where(visible[None], scores.reshape(per_kv, half_rows, window), MASKED)
            row_max = jnp.max(masked, axis=2, keepdims=True)
            weights = jnp.exp2((masked - row_max) * exponent)
            sums = jnp.sum(weights, axis=2, keepdims=True)
            rounded = weights.astype(jnp.bfloat16).reshape(per_kv * half_rows, window)
            mixed = jnp.dot(rounded, value_win[:, lanes], preferred_element_type=jnp.float32)
            context = (mixed.reshape(per_kv, half_rows, DH) / sums).astype(jnp.bfloat16)
            for h in range(per_kv):
                cols = slice((group * per_kv + h) * DH, (group * per_kv + h + 1) * DH)
                context_ref[rows, cols] = context[h]
                added = (
                    residual_ref[rows, cols].astype(jnp.float32) + context[h].astype(jnp.float32)
                ).astype(jnp.bfloat16)
                put(rows, group * per_kv + h, added)
                wide = added.astype(jnp.float32)
                squares = squares + wide * wide
        mean_square = jnp.sum(squares, axis=1, keepdims=True) * (1.0 / row_width)
        inverse = lax.rsqrt(mean_square + epsilon)
        inverse_ref[rows, :] = jnp.broadcast_to(inverse, (half_rows, DH))
        for ref in layer_refs[1:]:
            for left in range(0, ref.shape[1], DH):
                cols = slice(left, left + DH)
                ref[rows, cols] = (ref[rows, cols].astype(jnp.float32) * inverse).astype(jnp.bfloat16)


def attend(lengths, queries, residual, pairs, groups, stays):
    tok_rows, _ = queries.shape
    longest = tok_rows * groups // 4
    pair_width = pairs[0].shape[1]
    shape = pltpu.VMEM(queries.shape, jnp.bfloat16)
    return pl.pallas_call(
        functools.partial(attend_kernel, groups, longest, 1.0 / math.sqrt(DH), stays),
        out_shape=(
            shape,
            pltpu.VMEM((tok_rows, DH), jnp.float32),
            *[pltpu.VMEM((tok_rows, DH * len(heads)), jnp.bfloat16) for heads in stays],
        ),
        in_specs=[FAR] + [WHOLE] * (2 + len(pairs)),
        out_specs=(WHOLE,) * (2 + len(stays)),
        scratch_shapes=[
            pltpu.VMEM((groups, tok_rows, pair_width), jnp.bfloat16),
            pltpu.SMEM(lengths.shape, jnp.int32),
            pltpu.SemaphoreType.DMA,
        ],
        compiler_params=budget(16),
        name="attend",
    )(far(lengths), *[near(array) for array in (queries, residual, *pairs)])


def project_kernel(places, scaled, layer_ref, *refs):
    piece_refs = refs[: len(places)]
    *rest, out_ref = refs[len(places) :]
    depth = layer_ref.shape[1] // (lax.axis_size("seq") * lax.axis_size("exp"))
    seq, core = lax.axis_index("seq"), lax.axis_index("exp")
    total = rest[0][...] if len(rest) > scaled else None
    for (bit, kind, first), piece_ref in zip(places, piece_refs):
        rows = piece_ref.shape[0]
        column = ((seq ^ bit) * 2 + (core ^ kind)) * depth + first
        part = jnp.dot(
            layer_ref[:, pl.ds(pl.multiple_of(column, DH), rows)], piece_ref[...], preferred_element_type=jnp.float32
        )
        total = part if total is None else total + part
    if scaled:
        for left in range(0, total.shape[1], DH):
            cols = slice(left, left + DH)
            out_ref[:, cols] = (total[:, cols] * rest[-1][...]).astype(jnp.bfloat16)
    else:
        out_ref[...] = total


def project(layer, held, so_far=None, inverse=None):
    places = tuple(held)
    scaled = inverse is not None
    blocks = [held[place] for place in places]
    extra = [array for array in (so_far, inverse) if array is not None]
    shape = (layer.shape[0], blocks[0].shape[1])
    return pl.pallas_call(
        functools.partial(project_kernel, places, scaled),
        out_shape=pltpu.VMEM(shape, jnp.bfloat16 if scaled else jnp.float32),
        in_specs=[WHOLE] * (1 + len(blocks) + len(extra)),
        out_specs=WHOLE,
        compiler_params=budget(8),
        name="project",
    )(*[near(array) for array in (layer, *blocks, *extra)])


def gather_square(block, relays):
    early, late = {}, {}

    def hold(held, bit, first, piece):
        held[bit, 0, first] = piece
        held[bit, 1, first] = exchanged(piece, "exp", 1)

    hold(early, 0, 0, block)
    sides = {}
    for bit in (1, 2):
        sides[bit] = exchanged(block, "seq", bit)
        hold(early, bit, 0, sides[bit])
    part = block.shape[0] // len(relays)
    for index, bit in enumerate(relays):
        start = index * part
        corner = exchanged(sides[bit][start : start + part], "seq", 3 - bit)
        hold(late, 3, start, corner)
    return early, late


def square_of_chips(queries, key_rows, value_rows, residual, lengths, norm_gain, weight):
    pair, half, leaves, stays = prepare(key_rows, value_rows, norm_gain, weight, 2)
    leaves = shifted(leaves, -1)
    leaves_early, leaves_late = gather_square(leaves, (1, 2))
    stays_early, stays_late = gather_square(stays, (2,))
    pairs = [pair, exchanged(pair, "seq", 1)]
    pairs.append(exchanged(half, "seq", 2))
    pairs.append(exchanged(half, "seq", 3))
    queries, residual = fetch(queries, residual)
    per_block = weight.shape[0] // DH
    heads = range(queries.shape[1] // DH)
    parts = [[head for head in heads if (head % per_block < per_block // 2) == first] for first in (True, False)]
    context, inverse, layer, normed = attend(
        lengths, queries, residual, pairs, lax.axis_size("seq"), parts
    )
    context = store(context)
    received = shifted(normed, 1)
    so_far = project(layer, leaves_early)
    projected = project(layer, leaves_late, so_far, inverse)
    arrived = shifted(projected, 1)
    total = project(received, {**stays_early, **stays_late})
    return context, (arrived.astype(jnp.float32) + total).astype(jnp.bfloat16)


def any_mesh(queries, key_rows, value_rows, residual, lengths, norm_gain, weight):
    pair, _, part = prepare(key_rows, value_rows, norm_gain, weight, 1)
    pairs = [lax.all_gather(pair, "seq", axis=0, tiled=True)]
    heads = [list(range(queries.shape[1] // DH))]
    context, inverse, layer = attend(lengths, queries, residual, pairs, lax.axis_size("seq"), heads)
    every = lax.all_gather(shifted(part, -1), ("seq", "exp"), axis=0, tiled=True)
    total = jnp.dot(layer, every, preferred_element_type=jnp.float32)
    return context, shifted((total * inverse[:, :1]).astype(jnp.bfloat16), 1)


def is_square(sizes):
    return sizes["seq"] == 4 and sizes["exp"] == 2


def on_device(queries, key_rows, value_rows, residual, doc_lengths, norm_gain, kv_weight):
    square = is_square({axis: lax.axis_size(axis) for axis in ("seq", "exp")})
    context, kv_next = (square_of_chips if square else any_mesh)(
        queries[0, 0], key_rows[0, 0], value_rows[0, 0], residual[0, 0], doc_lengths[0], norm_gain, kv_weight[0]
    )
    return context[None, None], kv_next[None, None]


def solution(mesh):
    rows = P("pipe", "exp", "seq", None)
    return jax.shard_map(
        on_device,
        mesh=mesh,
        in_specs=(rows, rows, rows, rows, P("pipe", "exp", None), P("pipe", None), P("pipe", ("seq", "exp"), None)),
        out_specs=(rows, rows),
        check_vma=False,
    )
```

```python
import functools
import math

import jax
import jax.numpy as jnp
from jax import lax
from jax.experimental import pallas as pl
from jax.experimental.pallas import tpu as pltpu
from jax.sharding import PartitionSpec as P


DH = 128


epsilon = 1e-06
MASKED = -1e30
FEWER = 96

WHOLE = pl.BlockSpec(memory_space=pltpu.VMEM)
FAR = pl.BlockSpec(memory_space=pltpu.HBM)


def near(array):
    return pltpu.with_memory_space_constraint(array, pltpu.VMEM)


def far(array):
    return pltpu.with_memory_space_constraint(array, pltpu.HBM)


def budget(mebibytes):
    return pltpu.CompilerParams(vmem_limit_bytes=mebibytes << 20)


def shifted(block, distance):
    devices = range(lax.axis_size("pipe"))
    route = [(i - distance, i) for i in devices if i - distance in devices]
    return lax.ppermute(block, "pipe", route)


def paired(block, first):
    sections, cores = lax.axis_size("pipe"), lax.axis_size("exp")
    route = []
    for section in range(sections):
        other = section + 1 if (section - first) % 2 == 0 else section - 1
        for core in range(cores):
            target = other * cores + core if 0 <= other < sections else section * cores + (core ^ 1)
            route.append((section * cores + core, target))
    return lax.ppermute(block, ("pipe", "exp"), route)


def exchanged(block, axis, bit):
    return lax.ppermute(block, axis, [(i, i ^ bit) for i in range(lax.axis_size(axis))])


def run_copies(copies):
    for copy in copies:
        copy.start()
    for copy in copies:
        copy.wait()


def sent_half(device, groups):
    return (device >= groups // 2).astype(jnp.int32)


def prepare_kernel(key_ref, value_ref, gain_ref, weight_ref, pair_ref, half_ref, *refs):
    piece_refs, (weight, gain, sems) = refs[:-3], refs[-3:]
    half = half_ref.shape[0]
    sent = pl.ds(pl.multiple_of(sent_half(lax.axis_index("seq"), lax.axis_size("seq")) * half, half), half)
    width = key_ref.shape[1]
    depth = weight_ref.shape[0]
    at = (lax.axis_index("seq") * lax.axis_size("exp") + lax.axis_index("exp")) * depth
    run_copies(
        [
            pltpu.make_async_copy(weight_ref, weight, sems.at[0]),
            pltpu.make_async_copy(gain_ref, gain, sems.at[1]),
            pltpu.make_async_copy(key_ref, pair_ref.at[:, :width], sems.at[2]),
            pltpu.make_async_copy(value_ref, pair_ref.at[:, width:], sems.at[3]),
            pltpu.make_async_copy(key_ref.at[sent], half_ref.at[:, :width], sems.at[4]),
            pltpu.make_async_copy(value_ref.at[sent], half_ref.at[:, width:], sems.at[5]),
        ]
    )
    if depth % DH:
        wide = gain[...]
        place = lax.broadcasted_iota(jnp.int32, (depth, wide.shape[1]), 0) + at
        here = place == lax.broadcasted_iota(jnp.int32, place.shape, 1)
        column = jnp.sum(jnp.where(here, wide, 0.0), axis=1, keepdims=True)
    else:
        wide = gain[:, pl.ds(pl.multiple_of(at, depth), depth)]
        column = jnp.transpose(jnp.broadcast_to(wide, (DH, depth)))
    rows = depth // len(piece_refs)
    for index, piece_ref in enumerate(piece_refs):
        part = slice(index * rows, (index + 1) * rows)
        for left in range(0, weight.shape[1], DH):
            cols = slice(left, left + DH)
            piece_ref[:, cols] = (weight[part, cols].astype(jnp.float32) * column[part]).astype(jnp.bfloat16)


def prepare(key_rows, value_rows, norm_gain, weight, pieces):
    rows, width = key_rows.shape
    depth, cols = weight.shape
    piece = pltpu.VMEM((depth // pieces, cols), weight.dtype)
    return pl.pallas_call(
        prepare_kernel,
        out_shape=(
            pltpu.VMEM((rows, 2 * width), key_rows.dtype),
            pltpu.VMEM((rows // 2, 2 * width), key_rows.dtype),
            *[piece] * pieces,
        ),
        in_specs=[FAR] * 4,
        out_specs=(WHOLE,) * (2 + pieces),
        scratch_shapes=[
            pltpu.VMEM((depth, cols), weight.dtype),
            pltpu.VMEM(norm_gain.shape, jnp.float32),
            pltpu.SemaphoreType.DMA((6,)),
        ],
        compiler_params=budget(6),
        name="prepare",
    )(*[far(array) for array in (key_rows, value_rows, norm_gain, weight)])


def fetch_kernel(*refs):
    count = (len(refs) - 1) // 2
    sems = refs[-1]
    run_copies(
        [pltpu.make_async_copy(refs[i], refs[count + i], sems.at[i]) for i in range(count)]
    )


def fetch(*arrays):
    return pl.pallas_call(
        fetch_kernel,
        out_shape=tuple(pltpu.VMEM(array.shape, array.dtype) for array in arrays),
        in_specs=[FAR] * len(arrays),
        out_specs=(WHOLE,) * len(arrays),
        scratch_shapes=[pltpu.SemaphoreType.DMA((len(arrays),))],
        compiler_params=budget(4),
        name="fetch",
    )(*[far(array) for array in arrays])


def store_kernel(near_ref, far_ref, sem):
    run_copies([pltpu.make_async_copy(near_ref, far_ref, sem)])


def store(array):
    return pl.pallas_call(
        store_kernel,
        out_shape=jax.ShapeDtypeStruct(array.shape, array.dtype),
        in_specs=[WHOLE],
        out_specs=FAR,
        scratch_shapes=[pltpu.SemaphoreType.DMA],
        compiler_params=budget(2),
        name="store",
    )(near(array))


def attend_kernel(groups, longest, score_scale, stays, far_lengths_ref, query_ref, residual_ref, *refs):
    pair_refs, outs = refs[: -len(stays) - 5], refs[-len(stays) - 5 :]
    context_ref, inverse_ref, *layer_refs, every, lengths_ref, sem = outs
    lengths_copy = pltpu.make_async_copy(far_lengths_ref, lengths_ref, sem)
    lengths_copy.start()
    tok_rows, row_width = query_ref.shape
    half_rows = tok_rows // 2
    kv_width = every.shape[2] // 2
    kv_heads = kv_width // DH
    per_kv = row_width // DH // kv_heads
    window = longest + half_rows
    blocks = window // half_rows
    own = lax.axis_index("seq")
    if len(pair_refs) == 1:
        every[...] = pair_refs[0][...].reshape(every.shape)
    else:
        for bit, pair_ref in enumerate(pair_refs):
            sender, rows = own ^ bit, pair_ref.shape[0]
            if rows == tok_rows:
                every[sender] = pair_ref[...]
            else:
                at = pl.multiple_of(sent_half(sender, groups) * rows, rows)
                every[sender, pl.ds(at, rows), :] = pair_ref[...]
    lengths_copy.wait()
    bounds = []
    total = jnp.int32(0)
    for doc in range(lengths_ref.shape[1]):
        total = total + lengths_ref[0, doc]
        bounds.append(total)
    exponent = score_scale * math.log2(math.e)
    places = {head: (ref, at) for ref, heads in zip(layer_refs, stays) for at, head in enumerate(heads)}

    def put(rows, head, block):
        ref, at = places[head]
        ref[rows, at * DH : (at + 1) * DH] = block

    for run in range(2):
        block = own if run == 0 else 2 * groups - 1 - own
        first_pos = block * half_rows
        rows = slice(run * half_rows, (run + 1) * half_rows)
        query_pos = first_pos + lax.broadcasted_iota(jnp.int32, (half_rows, window), 0)
        key_pos = first_pos + half_rows - window + lax.broadcasted_iota(jnp.int32, (half_rows, window), 1)
        doc_start = jnp.zeros((half_rows, window), jnp.int32)
        for bound in bounds:
            doc_start = jnp.where(bound <= query_pos, bound, doc_start)
        visible = (doc_start <= key_pos) & (key_pos <= query_pos)
        key_parts, value_parts = [], []
        for back in range(blocks - 1, -1, -1):
            natural = jnp.maximum(block - back, 0)
            second = natural >= groups
            owner = jnp.where(second, 2 * groups - 1 - natural, natural)
            offset = jnp.where(second, half_rows, 0)
            part = every[owner, pl.ds(pl.multiple_of(offset, half_rows), half_rows), :]
            key_parts.append(part[:, :kv_width])
            value_parts.append(part[:, kv_width:])
        key_win = jnp.concatenate(key_parts, axis=0)
        value_win = jnp.concatenate(value_parts, axis=0)
        squares = jnp.zeros((half_rows, DH), jnp.float32)
        for group in range(kv_heads):
            lanes = slice(group * DH, (group + 1) * DH)
            query_stack = jnp.concatenate(
                [
                    query_ref[rows, (group * per_kv + h) * DH : (group * per_kv + h + 1) * DH]
                    for h in range(per_kv)
                ],
                axis=0,
            )
            scores = lax.dot_general(
                query_stack, key_win[:, lanes], (((1,), (1,)), ((), ())), preferred_element_type=jnp.float32
            )
            masked = jnp.where(visible[None], scores.reshape(per_kv, half_rows, window), MASKED)
            row_max = jnp.max(masked, axis=2, keepdims=True)
            weights = jnp.exp2((masked - row_max) * exponent)
            sums = jnp.sum(weights, axis=2, keepdims=True)
            rounded = weights.astype(jnp.bfloat16).reshape(per_kv * half_rows, window)
            mixed = jnp.dot(rounded, value_win[:, lanes], preferred_element_type=jnp.float32)
            context = (mixed.reshape(per_kv, half_rows, DH) / sums).astype(jnp.bfloat16)
            for h in range(per_kv):
                cols = slice((group * per_kv + h) * DH, (group * per_kv + h + 1) * DH)
                context_ref[rows, cols] = context[h]
                added = (
                    residual_ref[rows, cols].astype(jnp.float32) + context[h].astype(jnp.float32)
                ).astype(jnp.bfloat16)
                put(rows, group * per_kv + h, added)
                wide = added.astype(jnp.float32)
                squares = squares + wide * wide
        mean_square = jnp.sum(squares, axis=1, keepdims=True) * (1.0 / row_width)
        inverse = lax.rsqrt(mean_square + epsilon)
        inverse_ref[rows, :] = jnp.broadcast_to(inverse, (half_rows, DH))
        for ref in layer_refs[1:]:
            for left in range(0, ref.shape[1], DH):
                cols = slice(left, left + DH)
                ref[rows, cols] = (ref[rows, cols].astype(jnp.float32) * inverse).astype(jnp.bfloat16)


def attend(lengths, queries, residual, pairs, groups, stays):
    tok_rows, _ = queries.shape
    longest = tok_rows * groups // 4
    pair_width = pairs[0].shape[1]
    shape = pltpu.VMEM(queries.shape, jnp.bfloat16)
    return pl.pallas_call(
        functools.partial(attend_kernel, groups, longest, 1.0 / math.sqrt(DH), stays),
        out_shape=(
            shape,
            pltpu.VMEM((tok_rows, DH), jnp.float32),
            *[pltpu.VMEM((tok_rows, DH * len(heads)), jnp.bfloat16) for heads in stays],
        ),
        in_specs=[FAR] + [WHOLE] * (2 + len(pairs)),
        out_specs=(WHOLE,) * (2 + len(stays)),
        scratch_shapes=[
            pltpu.VMEM((groups, tok_rows, pair_width), jnp.bfloat16),
            pltpu.SMEM(lengths.shape, jnp.int32),
            pltpu.SemaphoreType.DMA,
        ],
        compiler_params=budget(16),
        name="attend",
    )(far(lengths), *[near(array) for array in (queries, residual, *pairs)])


def project_kernel(places, scaled, sides, *refs):
    layer_refs, refs = refs[:sides], refs[sides:]
    layer_ref = layer_refs[0]
    odd = lax.axis_index("pipe") % 2 == 1
    piece_refs = refs[: len(places)]
    *rest, out_ref = refs[len(places) :]
    depth = layer_ref.shape[1] // (lax.axis_size("seq") * lax.axis_size("exp"))
    seq, core = lax.axis_index("seq"), lax.axis_index("exp")
    total = rest[0][...] if len(rest) > scaled else None
    blocks = {}
    for (bit, kind, _), piece_ref in zip(places, piece_refs):
        blocks.setdefault((bit, kind), []).append(piece_ref[...])
    for (bit, kind), pieces in blocks.items():
        column = ((seq ^ bit) * 2 + (core ^ kind)) * depth
        cols = pl.ds(pl.multiple_of(column, DH), depth)
        block = layer_ref[:, cols]
        if sides == 2:
            block = jnp.where(odd, block, layer_refs[1][:, cols])
        part = jnp.dot(block, jnp.concatenate(pieces, axis=0), preferred_element_type=jnp.float32)
        total = part if total is None else total + part
    if scaled:
        for left in range(0, total.shape[1], DH):
            cols = slice(left, left + DH)
            out_ref[:, cols] = (total[:, cols] * rest[-1][...]).astype(jnp.bfloat16)
    else:
        out_ref[...] = total


def project(layer, held, so_far=None, inverse=None):
    layers = layer if isinstance(layer, list) else [layer]
    places = tuple(sorted(held))
    scaled = inverse is not None
    blocks = [held[place] for place in places]
    extra = [array for array in (so_far, inverse) if array is not None]
    shape = (layers[0].shape[0], blocks[0].shape[1])
    return pl.pallas_call(
        functools.partial(project_kernel, places, scaled, len(layers)),
        out_shape=pltpu.VMEM(shape, jnp.bfloat16 if scaled else jnp.float32),
        in_specs=[WHOLE] * (len(layers) + len(blocks) + len(extra)),
        out_specs=WHOLE,
        compiler_params=budget(8),
        name="project",
    )(*[near(array) for array in (*layers, *blocks, *extra)])


def finish_kernel(total_ref, *refs):
    *arrived_refs, far_ref, near_ref, sem = refs
    section = lax.axis_index("pipe")
    arrived = arrived_refs[0][...].astype(jnp.float32)
    if len(arrived_refs) == 2:
        arrived = jnp.where(section % 2 == 1, arrived, arrived_refs[1][...].astype(jnp.float32))
    summed = (arrived + total_ref[...]).astype(jnp.bfloat16)
    near_ref[...] = jnp.where(section > 0, summed, jnp.zeros_like(summed))
    run_copies([pltpu.make_async_copy(near_ref, far_ref, sem)])


def finish(total, *arrived):
    shape = jax.ShapeDtypeStruct(total.shape, jnp.bfloat16)
    return pl.pallas_call(
        finish_kernel,
        out_shape=shape,
        in_specs=[WHOLE] * (1 + len(arrived)),
        out_specs=FAR,
        scratch_shapes=[pltpu.VMEM(shape.shape, shape.dtype), pltpu.SemaphoreType.DMA],
        compiler_params=budget(2),
        name="finish",
    )(*[near(array) for array in (total, *arrived)])


def gather_square(block, relays):
    early, late = {}, {}

    def hold(held, bit, first, piece):
        held[bit, 0, first] = piece
        held[bit, 1, first] = exchanged(piece, "exp", 1)

    hold(early, 0, 0, block)
    sides = {}
    for bit in (1, 2):
        sides[bit] = exchanged(block, "seq", bit)
        hold(early, bit, 0, sides[bit])
    start = 0
    for bit, rows in relays:
        corner = exchanged(sides[bit][start : start + rows], "seq", 3 - bit)
        hold(late, 3, start, corner)
        start += rows
    return early, late


def square_of_chips(queries, key_rows, value_rows, residual, lengths, norm_gain, weight):
    pair, half, leaves, stays = prepare(key_rows, value_rows, norm_gain, weight, 2)
    leaves = shifted(leaves, -1)
    rows = leaves.shape[0]
    leaves_early, leaves_late = gather_square(leaves, ((1, rows - FEWER), (2, FEWER)))
    stays_early, stays_late = gather_square(stays, ((2, rows),))
    pairs = [pair, exchanged(pair, "seq", 1)]
    pairs.append(exchanged(half, "seq", 2))
    pairs.append(exchanged(half, "seq", 3))
    queries, residual = fetch(queries, residual)
    per_block = weight.shape[0] // DH
    heads = range(queries.shape[1] // DH)
    parts = [[head for head in heads if (head % per_block < per_block // 2) == first] for first in (True, False)]
    context, inverse, layer, normed = attend(
        lengths, queries, residual, pairs, lax.axis_size("seq"), parts
    )
    context = store(context)
    received = []
    for first in (0, 1):
        received.append(paired(normed, first))
    so_far = project(layer, leaves_early)
    projected = project(layer, leaves_late, so_far, inverse)
    arrived = []
    for first in (0, 1):
        arrived.append(paired(projected, first))
    total = project(received, {**stays_early, **stays_late})
    return context, finish(total, *arrived)


def any_mesh(queries, key_rows, value_rows, residual, lengths, norm_gain, weight):
    pair, _, part = prepare(key_rows, value_rows, norm_gain, weight, 1)
    pairs = [lax.all_gather(pair, "seq", axis=0, tiled=True)]
    heads = [list(range(queries.shape[1] // DH))]
    context, inverse, layer = attend(lengths, queries, residual, pairs, lax.axis_size("seq"), heads)
    every = lax.all_gather(shifted(part, -1), ("seq", "exp"), axis=0, tiled=True)
    total = jnp.dot(layer, every, preferred_element_type=jnp.float32)
    return context, shifted((total * inverse[:, :1]).astype(jnp.bfloat16), 1)


def is_square(sizes):
    return sizes["seq"] == 4 and sizes["exp"] == 2


def on_device(queries, key_rows, value_rows, residual, doc_lengths, norm_gain, kv_weight):
    square = is_square({axis: lax.axis_size(axis) for axis in ("seq", "exp")})
    context, kv_next = (square_of_chips if square else any_mesh)(
        queries[0, 0], key_rows[0, 0], value_rows[0, 0], residual[0, 0], doc_lengths[0], norm_gain, kv_weight[0]
    )
    return context[None, None], kv_next[None, None]


def solution(mesh):
    rows = P("pipe", "exp", "seq", None)
    return jax.shard_map(
        on_device,
        mesh=mesh,
        in_specs=(rows, rows, rows, rows, P("pipe", "exp", None), P("pipe", None), P("pipe", ("seq", "exp"), None)),
        out_specs=(rows, rows),
        check_vma=False,
    )
```

```python
import functools
import math

import jax
import jax.numpy as jnp
from jax import lax
from jax.experimental import pallas as pl
from jax.experimental.pallas import tpu as pltpu
from jax.sharding import PartitionSpec as P


DH = 128


epsilon = 1e-06
MASKED = -1e30
FEWER = 112

WHOLE = pl.BlockSpec(memory_space=pltpu.VMEM)
FAR = pl.BlockSpec(memory_space=pltpu.HBM)


def near(array):
    return pltpu.with_memory_space_constraint(array, pltpu.VMEM)


def far(array):
    return pltpu.with_memory_space_constraint(array, pltpu.HBM)


def budget(mebibytes):
    return pltpu.CompilerParams(vmem_limit_bytes=mebibytes << 20)


def shifted(block, distance):
    devices = range(lax.axis_size("pipe"))
    route = [(i - distance, i) for i in devices if i - distance in devices]
    return lax.ppermute(block, "pipe", route)


def paired(block, first):
    sections, cores = lax.axis_size("pipe"), lax.axis_size("exp")
    route = []
    for section in range(sections):
        other = section + 1 if (section - first) % 2 == 0 else section - 1
        for core in range(cores):
            target = other * cores + core if 0 <= other < sections else section * cores + (core ^ 1)
            route.append((section * cores + core, target))
    return lax.ppermute(block, ("pipe", "exp"), route)


def exchanged(block, axis, bit):
    return lax.ppermute(block, axis, [(i, i ^ bit) for i in range(lax.axis_size(axis))])


def run_copies(copies):
    for copy in copies:
        copy.start()
    for copy in copies:
        copy.wait()


def sent_half(device, groups):
    return (device >= groups // 2).astype(jnp.int32)


def prepare_kernel(key_ref, value_ref, gain_ref, weight_ref, pair_ref, half_ref, *refs):
    piece_refs, (weight, gain, sems) = refs[:-3], refs[-3:]
    half = half_ref.shape[0]
    sent = pl.ds(pl.multiple_of(sent_half(lax.axis_index("seq"), lax.axis_size("seq")) * half, half), half)
    width = key_ref.shape[1]
    depth = weight_ref.shape[0]
    at = (lax.axis_index("seq") * lax.axis_size("exp") + lax.axis_index("exp")) * depth
    loads = [pltpu.make_async_copy(gain_ref, gain, sems.at[1]), pltpu.make_async_copy(weight_ref, weight, sems.at[0])]
    for load in loads:
        load.start()
    rest = (
        [
            pltpu.make_async_copy(key_ref, pair_ref.at[:, :width], sems.at[2]),
            pltpu.make_async_copy(value_ref, pair_ref.at[:, width:], sems.at[3]),
            pltpu.make_async_copy(key_ref.at[sent], half_ref.at[:, :width], sems.at[4]),
            pltpu.make_async_copy(value_ref.at[sent], half_ref.at[:, width:], sems.at[5]),
        ]
    )
    for copy in rest:
        copy.start()
    loads[0].wait()
    if depth % DH:
        wide = gain[...]
        place = lax.broadcasted_iota(jnp.int32, (depth, wide.shape[1]), 0) + at
        here = place == lax.broadcasted_iota(jnp.int32, place.shape, 1)
        column = jnp.sum(jnp.where(here, wide, 0.0), axis=1, keepdims=True)
    else:
        wide = gain[:, pl.ds(pl.multiple_of(at, depth), depth)]
        column = jnp.transpose(jnp.broadcast_to(wide, (DH, depth)))
    loads[1].wait()
    rows = depth // len(piece_refs)
    for index, piece_ref in enumerate(piece_refs):
        part = slice(index * rows, (index + 1) * rows)
        for left in range(0, weight.shape[1], DH):
            cols = slice(left, left + DH)
            piece_ref[:, cols] = (weight[part, cols].astype(jnp.float32) * column[part]).astype(jnp.bfloat16)
    for copy in rest:
        copy.wait()


def prepare(key_rows, value_rows, norm_gain, weight, pieces):
    rows, width = key_rows.shape
    depth, cols = weight.shape
    piece = pltpu.VMEM((depth // pieces, cols), weight.dtype)
    return pl.pallas_call(
        prepare_kernel,
        out_shape=(
            pltpu.VMEM((rows, 2 * width), key_rows.dtype),
            pltpu.VMEM((rows // 2, 2 * width), key_rows.dtype),
            *[piece] * pieces,
        ),
        in_specs=[FAR] * 4,
        out_specs=(WHOLE,) * (2 + pieces),
        scratch_shapes=[
            pltpu.VMEM((depth, cols), weight.dtype),
            pltpu.VMEM(norm_gain.shape, jnp.float32),
            pltpu.SemaphoreType.DMA((6,)),
        ],
        compiler_params=budget(6),
        name="prepare",
    )(*[far(array) for array in (key_rows, value_rows, norm_gain, weight)])


def fetch_kernel(*refs):
    count = (len(refs) - 1) // 2
    sems = refs[-1]
    run_copies(
        [pltpu.make_async_copy(refs[i], refs[count + i], sems.at[i]) for i in range(count)]
    )


def fetch(*arrays):
    return pl.pallas_call(
        fetch_kernel,
        out_shape=tuple(pltpu.VMEM(array.shape, array.dtype) for array in arrays),
        in_specs=[FAR] * len(arrays),
        out_specs=(WHOLE,) * len(arrays),
        scratch_shapes=[pltpu.SemaphoreType.DMA((len(arrays),))],
        compiler_params=budget(4),
        name="fetch",
    )(*[far(array) for array in arrays])


def store_kernel(near_ref, far_ref, sem):
    run_copies([pltpu.make_async_copy(near_ref, far_ref, sem)])


def store(array):
    return pl.pallas_call(
        store_kernel,
        out_shape=jax.ShapeDtypeStruct(array.shape, array.dtype),
        in_specs=[WHOLE],
        out_specs=FAR,
        scratch_shapes=[pltpu.SemaphoreType.DMA],
        compiler_params=budget(2),
        name="store",
    )(near(array))


def attend_kernel(groups, longest, score_scale, stays, far_lengths_ref, query_ref, residual_ref, *refs):
    pair_refs, outs = refs[: -len(stays) - 5], refs[-len(stays) - 5 :]
    context_ref, inverse_ref, *layer_refs, every, lengths_ref, sem = outs
    lengths_copy = pltpu.make_async_copy(far_lengths_ref, lengths_ref, sem)
    lengths_copy.start()
    tok_rows, row_width = query_ref.shape
    half_rows = tok_rows // 2
    kv_width = every.shape[2] // 2
    kv_heads = kv_width // DH
    per_kv = row_width // DH // kv_heads
    window = longest + half_rows
    blocks = window // half_rows
    own = lax.axis_index("seq")
    if len(pair_refs) == 1:
        every[...] = pair_refs[0][...].reshape(every.shape)
    else:
        for bit, pair_ref in enumerate(pair_refs):
            sender, rows = own ^ bit, pair_ref.shape[0]
            if rows == tok_rows:
                every[sender] = pair_ref[...]
            else:
                at = pl.multiple_of(sent_half(sender, groups) * rows, rows)
                every[sender, pl.ds(at, rows), :] = pair_ref[...]
    lengths_copy.wait()
    bounds = []
    total = jnp.int32(0)
    for doc in range(lengths_ref.shape[1]):
        total = total + lengths_ref[0, doc]
        bounds.append(total)
    exponent = score_scale * math.log2(math.e)
    places = {head: (ref, at) for ref, heads in zip(layer_refs, stays) for at, head in enumerate(heads)}

    def put(rows, head, block):
        ref, at = places[head]
        ref[rows, at * DH : (at + 1) * DH] = block

    for run in range(2):
        block = own if run == 0 else 2 * groups - 1 - own
        first_pos = block * half_rows
        rows = slice(run * half_rows, (run + 1) * half_rows)
        query_pos = first_pos + lax.broadcasted_iota(jnp.int32, (half_rows, window), 0)
        key_pos = first_pos + half_rows - window + lax.broadcasted_iota(jnp.int32, (half_rows, window), 1)
        doc_start = jnp.zeros((half_rows, window), jnp.int32)
        for bound in bounds:
            doc_start = jnp.where(bound <= query_pos, bound, doc_start)
        visible = (doc_start <= key_pos) & (key_pos <= query_pos)
        key_parts, value_parts = [], []
        for back in range(blocks - 1, -1, -1):
            natural = jnp.maximum(block - back, 0)
            second = natural >= groups
            owner = jnp.where(second, 2 * groups - 1 - natural, natural)
            offset = jnp.where(second, half_rows, 0)
            part = every[owner, pl.ds(pl.multiple_of(offset, half_rows), half_rows), :]
            key_parts.append(part[:, :kv_width])
            value_parts.append(part[:, kv_width:])
        key_win = jnp.concatenate(key_parts, axis=0)
        value_win = jnp.concatenate(value_parts, axis=0)
        squares = jnp.zeros((half_rows, DH), jnp.float32)
        for group in range(kv_heads):
            lanes = slice(group * DH, (group + 1) * DH)
            query_stack = jnp.concatenate(
                [
                    query_ref[rows, (group * per_kv + h) * DH : (group * per_kv + h + 1) * DH]
                    for h in range(per_kv)
                ],
                axis=0,
            )
            scores = lax.dot_general(
                query_stack, key_win[:, lanes], (((1,), (1,)), ((), ())), preferred_element_type=jnp.float32
            )
            masked = jnp.where(visible[None], scores.reshape(per_kv, half_rows, window), MASKED)
            row_max = jnp.max(masked, axis=2, keepdims=True)
            weights = jnp.exp2((masked - row_max) * exponent)
            sums = jnp.sum(weights, axis=2, keepdims=True)
            rounded = weights.astype(jnp.bfloat16).reshape(per_kv * half_rows, window)
            mixed = jnp.dot(rounded, value_win[:, lanes], preferred_element_type=jnp.float32)
            context = (mixed.reshape(per_kv, half_rows, DH) / sums).astype(jnp.bfloat16)
            for h in range(per_kv):
                cols = slice((group * per_kv + h) * DH, (group * per_kv + h + 1) * DH)
                context_ref[rows, cols] = context[h]
                added = (
                    residual_ref[rows, cols].astype(jnp.float32) + context[h].astype(jnp.float32)
                ).astype(jnp.bfloat16)
                put(rows, group * per_kv + h, added)
                wide = added.astype(jnp.float32)
                squares = squares + wide * wide
        mean_square = jnp.sum(squares, axis=1, keepdims=True) * (1.0 / row_width)
        inverse = lax.rsqrt(mean_square + epsilon)
        inverse_ref[rows, :] = jnp.broadcast_to(inverse, (half_rows, DH))
        for ref in layer_refs[1:]:
            for left in range(0, ref.shape[1], DH):
                cols = slice(left, left + DH)
                ref[rows, cols] = (ref[rows, cols].astype(jnp.float32) * inverse).astype(jnp.bfloat16)


def attend(lengths, queries, residual, pairs, groups, stays):
    tok_rows, _ = queries.shape
    longest = tok_rows * groups // 4
    pair_width = pairs[0].shape[1]
    shape = pltpu.VMEM(queries.shape, jnp.bfloat16)
    return pl.pallas_call(
        functools.partial(attend_kernel, groups, longest, 1.0 / math.sqrt(DH), stays),
        out_shape=(
            shape,
            pltpu.VMEM((tok_rows, DH), jnp.float32),
            *[pltpu.VMEM((tok_rows, DH * len(heads)), jnp.bfloat16) for heads in stays],
        ),
        in_specs=[FAR] + [WHOLE] * (2 + len(pairs)),
        out_specs=(WHOLE,) * (2 + len(stays)),
        scratch_shapes=[
            pltpu.VMEM((groups, tok_rows, pair_width), jnp.bfloat16),
            pltpu.SMEM(lengths.shape, jnp.int32),
            pltpu.SemaphoreType.DMA,
        ],
        compiler_params=budget(16),
        name="attend",
    )(far(lengths), *[near(array) for array in (queries, residual, *pairs)])


def project_kernel(places, scaled, sides, *refs):
    layer_refs, refs = refs[:sides], refs[sides:]
    layer_ref = layer_refs[0]
    odd = lax.axis_index("pipe") % 2 == 1
    piece_refs = refs[: len(places)]
    *rest, out_ref = refs[len(places) :]
    depth = layer_ref.shape[1] // (lax.axis_size("seq") * lax.axis_size("exp"))
    seq, core = lax.axis_index("seq"), lax.axis_index("exp")
    total = rest[0][...] if len(rest) > scaled else None
    blocks = {}
    for (bit, kind, _), piece_ref in zip(places, piece_refs):
        blocks.setdefault((bit, kind), []).append(piece_ref[...])
    for (bit, kind), pieces in blocks.items():
        column = ((seq ^ bit) * 2 + (core ^ kind)) * depth
        cols = pl.ds(pl.multiple_of(column, DH), depth)
        block = layer_ref[:, cols]
        if sides == 2:
            block = jnp.where(odd, block, layer_refs[1][:, cols])
        part = jnp.dot(block, jnp.concatenate(pieces, axis=0), preferred_element_type=jnp.float32)
        total = part if total is None else total + part
    if scaled:
        for left in range(0, total.shape[1], DH):
            cols = slice(left, left + DH)
            out_ref[:, cols] = (total[:, cols] * rest[-1][...]).astype(jnp.bfloat16)
    else:
        out_ref[...] = total


def project(layer, held, so_far=None, inverse=None):
    layers = layer if isinstance(layer, list) else [layer]
    places = tuple(sorted(held))
    scaled = inverse is not None
    blocks = [held[place] for place in places]
    extra = [array for array in (so_far, inverse) if array is not None]
    shape = (layers[0].shape[0], blocks[0].shape[1])
    return pl.pallas_call(
        functools.partial(project_kernel, places, scaled, len(layers)),
        out_shape=pltpu.VMEM(shape, jnp.bfloat16 if scaled else jnp.float32),
        in_specs=[WHOLE] * (len(layers) + len(blocks) + len(extra)),
        out_specs=WHOLE,
        compiler_params=budget(8),
        name="project",
    )(*[near(array) for array in (*layers, *blocks, *extra)])


def finish_kernel(total_ref, *refs):
    *arrived_refs, far_ref, near_ref, sem = refs
    section = lax.axis_index("pipe")
    arrived = arrived_refs[0][...].astype(jnp.float32)
    if len(arrived_refs) == 2:
        arrived = jnp.where(section % 2 == 1, arrived, arrived_refs[1][...].astype(jnp.float32))
    summed = (arrived + total_ref[...]).astype(jnp.bfloat16)
    near_ref[...] = jnp.where(section > 0, summed, jnp.zeros_like(summed))
    run_copies([pltpu.make_async_copy(near_ref, far_ref, sem)])


def finish(total, *arrived):
    shape = jax.ShapeDtypeStruct(total.shape, jnp.bfloat16)
    return pl.pallas_call(
        finish_kernel,
        out_shape=shape,
        in_specs=[WHOLE] * (1 + len(arrived)),
        out_specs=FAR,
        scratch_shapes=[pltpu.VMEM(shape.shape, shape.dtype), pltpu.SemaphoreType.DMA],
        compiler_params=budget(2),
        name="finish",
    )(*[near(array) for array in (total, *arrived)])


def gather_square(block, relays):
    early, late = {}, {}

    def hold(held, bit, first, piece):
        held[bit, 0, first] = piece
        held[bit, 1, first] = exchanged(piece, "exp", 1)

    hold(early, 0, 0, block)
    sides = {}
    for bit in (1, 2):
        sides[bit] = exchanged(block, "seq", bit)
        hold(early, bit, 0, sides[bit])
    start = 0
    for bit, rows in relays:
        corner = exchanged(sides[bit][start : start + rows], "seq", 3 - bit)
        hold(late, 3, start, corner)
        start += rows
    return early, late


def square_of_chips(queries, key_rows, value_rows, residual, lengths, norm_gain, weight):
    pair, half, leaves, stays = prepare(key_rows, value_rows, norm_gain, weight, 2)
    leaves = shifted(leaves, -1)
    rows = leaves.shape[0]
    leaves_early, leaves_late = gather_square(leaves, ((2, rows - FEWER), (1, FEWER)))
    stays_early, stays_late = gather_square(stays, ((1, rows),))
    pairs = [pair, exchanged(pair, "seq", 1)]
    pairs.append(exchanged(half, "seq", 2))
    pairs.append(exchanged(half, "seq", 3))
    queries, residual = fetch(queries, residual)
    per_block = weight.shape[0] // DH
    heads = range(queries.shape[1] // DH)
    parts = [[head for head in heads if (head % per_block < per_block // 2) == first] for first in (True, False)]
    context, inverse, layer, normed = attend(
        lengths, queries, residual, pairs, lax.axis_size("seq"), parts
    )
    context = store(context)
    received = []
    for first in (0, 1):
        received.append(paired(normed, first))
    so_far = project(layer, leaves_early)
    projected = project(layer, leaves_late, so_far, inverse)
    arrived = []
    for first in (0, 1):
        arrived.append(paired(projected, first))
    total = project(received, {**stays_early, **stays_late})
    return context, finish(total, *arrived)


def any_mesh(queries, key_rows, value_rows, residual, lengths, norm_gain, weight):
    pair, _, part = prepare(key_rows, value_rows, norm_gain, weight, 1)
    pairs = [lax.all_gather(pair, "seq", axis=0, tiled=True)]
    heads = [list(range(queries.shape[1] // DH))]
    context, inverse, layer = attend(lengths, queries, residual, pairs, lax.axis_size("seq"), heads)
    every = lax.all_gather(shifted(part, -1), ("seq", "exp"), axis=0, tiled=True)
    total = jnp.dot(layer, every, preferred_element_type=jnp.float32)
    return context, shifted((total * inverse[:, :1]).astype(jnp.bfloat16), 1)


def is_square(sizes):
    return sizes["seq"] == 4 and sizes["exp"] == 2


def on_device(queries, key_rows, value_rows, residual, doc_lengths, norm_gain, kv_weight):
    square = is_square({axis: lax.axis_size(axis) for axis in ("seq", "exp")})
    context, kv_next = (square_of_chips if square else any_mesh)(
        queries[0, 0], key_rows[0, 0], value_rows[0, 0], residual[0, 0], doc_lengths[0], norm_gain, kv_weight[0]
    )
    return context[None, None], kv_next[None, None]


def solution(mesh):
    rows = P("pipe", "exp", "seq", None)
    return jax.shard_map(
        on_device,
        mesh=mesh,
        in_specs=(rows, rows, rows, rows, P("pipe", "exp", None), P("pipe", None), P("pipe", ("seq", "exp"), None)),
        out_specs=(rows, rows),
        check_vma=False,
    )
```
